512 devices in a mesh: seq: 64 (over z, y), chan: 8 (over x, core).
Axes of the slice: x: 4, y: 4, z: 16, core: 2. Of those that a mesh axis runs over, the one named last changes fastest.
Arguments:
- values: bfloat16 [16384, 4096], P('seq', 'chan'), may hold values from -6 to 6
- gates: bfloat16 [16384, 4096], P('seq', 'chan'), may hold values from -144 to 144
- filter_taps: bfloat16 [16384, 4096], P('seq', 'chan'), may hold values from -0.0625 to 0.0625, as said below
- skip_gain: float32 [4096], P('chan'), may hold values from -0.125 to 0.125
- out_weight: bfloat16 [4096, 2048], P('chan'), may hold values from -0.09375 to 0.09375
Outputs:
- projected: bfloat16 [2048, 16384], P('chan', 'seq')
The draws below stay inside these ranges and needn't reach their ends.
Inputs may be any that keep to these rules, and one draw needn't show every extreme that they name: `filter_taps`: a causal filter for each channel.
All inputs are finite; a program needn't handle non-finite values.
Results may differ from the reference program's by a relative error of at most 0.0049.
Values may be sent and summed in bfloat16 or wider, within the bound.
A program may use at most 64 MiB of HBM per device.

```python
import math
import jax
import jax.numpy as jnp
from jax import lax

D = 4096
DOUT = 2048
TOK_DEV = 256
TOKENS = 16384


tap_level = 0.03125


def draw_filter_taps(key, part):
    keys = jax.random.split(jax.random.fold_in(key, 17), 6)
    lag_blocks = TOKENS // TOK_DEV
    steps = jnp.arange(TOKENS, dtype=jnp.float32)[:, None]
    fast_tau = jnp.exp(jax.random.uniform(keys[0], (1, D), jnp.float32, math.log(30.0), math.log(TOKENS / 8.0)))
    fast_noise = jax.random.truncated_normal(keys[3], -4.0, 4.0, (TOKENS, D), jnp.float32)
    base_noise = jax.random.truncated_normal(keys[4], -4.0, 4.0, (TOKENS, D), jnp.float32)
    share = jnp.exp(jax.random.uniform(keys[1], (1, D), jnp.float32, math.log(0.1), math.log(0.5)))
    slow_tau = jnp.exp(jax.random.uniform(keys[2], (1, D), jnp.float32, math.log(0.5 * TOKENS), math.log(4.0 * TOKENS)))
    slow_noise = base_noise
    fast = jnp.exp(-steps / fast_tau) * jnp.sqrt(2.0 / fast_tau) * fast_noise
    slow = jnp.exp(-steps / slow_tau) * jnp.sqrt(2.0 / slow_tau) * slow_noise
    mixed = jnp.sqrt(1.0 - share) * fast + jnp.sqrt(share) * slow
    levels = jnp.exp(jax.random.uniform(keys[5], (lag_blocks, 1, D), jnp.float32, -0.5, 0.5))
    taps = (mixed.reshape(lag_blocks, TOK_DEV, D) * levels).reshape(TOKENS, D) * tap_level
    return taps.astype(jnp.bfloat16)


def shard_levels(stream_key, extent, cuts, least, top_value):
    gain, own = 1.0, jax.random.fold_in(stream_key, 6)
    for dim, blocks in cuts:
        draws = jnp.exp(jax.random.uniform(jax.random.fold_in(own, dim), (blocks,), jnp.float32, least / len(cuts), top_value / len(cuts)))
        gain = gain * jnp.repeat(draws, extent[dim] // blocks).reshape([-1 if axis == dim else 1 for axis in range(len(extent))])
    return gain


def bell_draw(key, extent, scale, reach, cuts=(), held_as=jnp.bfloat16):
    values = scale * jax.random.normal(key, extent, jnp.float32)
    if cuts:
        values = values * shard_levels(key, extent, cuts, -0.22, 0.18)
    return jnp.clip(values, -reach, reach).astype(held_as)


def setup_inputs(seed: int = 0) -> dict:
    splits = jax.random.split(jax.random.key(seed), 6)
    values = bell_draw(splits[0], (TOKENS, D), 1.0, 6.0, ((0, 64), (1, 8)))
    gates = bell_draw(splits[1], (TOKENS, D), 24.0, 144.0, ((0, 64), (1, 8)))
    filter_taps = draw_filter_taps(jax.random.fold_in(splits[5], 71), 0)
    skip_gain = bell_draw(splits[3], (D,), 0.03125, 0.125, ((0, 8),), jnp.float32)
    out_weight = bell_draw(splits[4], (D, DOUT), D ** -0.5, 0.09375, ((0, 8),))
    return {"values": values, "gates": gates, "filter_taps": filter_taps, "skip_gain": skip_gain, "out_weight": out_weight}


def reference(values, gates, filter_taps, skip_gain, out_weight):
    length = values.shape[0]
    width = values.shape[1]
    blocks = width // 128
    value_blocks = jnp.moveaxis(values.astype(jnp.float32).reshape(length, blocks, 128), 1, 0)
    filter_blocks = jnp.moveaxis(filter_taps.astype(jnp.float32).reshape(length, blocks, 128), 1, 0)

    def convolve(pair):
        signal, taps = pair
        signal_freq = jnp.fft.rfft(signal, n=2 * length, axis=0)
        taps_freq = jnp.fft.rfft(taps, n=2 * length, axis=0)
        return jnp.fft.irfft(signal_freq * taps_freq, n=2 * length, axis=0)[:length]

    conv_blocks = lax.map(convolve, (value_blocks, filter_blocks))
    conv = jnp.moveaxis(conv_blocks, 0, 1).reshape(length, width).astype(jnp.float32)
    gated = (gates.astype(jnp.float32) * (conv + skip_gain[None, :] * values.astype(jnp.float32))).astype(jnp.bfloat16)
    projected = lax.dot_general(out_weight, gated, (((0,), (1,)), ((), ())), preferred_element_type=jnp.float32)
    return projected.astype(jnp.bfloat16)
```

```python
import functools

import jax
import jax.numpy as jnp
import numpy as np
from jax import lax
from jax.experimental import pallas as pl
from jax.experimental.pallas import tpu as pltpu
from jax.sharding import PartitionSpec as P

MESH = pl.DeviceIdType.MESH
F32 = jnp.float32
BF16 = jnp.bfloat16


def split_table(table):
    high = table.astype(np.float32).astype(BF16)
    low = (table - high.astype(np.float64)).astype(np.float32).astype(BF16)
    return high, low


def tables(blocks, rows):
    ids = np.arange(blocks)
    turn = ids[:, None] * (2 * ids[None, :] + 1) % (4 * blocks) * (2 * np.pi / (4 * blocks))
    outer = np.concatenate([np.cos(turn).T, -np.sin(turn).T], axis=0)
    final = np.concatenate([np.cos(turn), -np.sin(turn)], axis=1) / (blocks * rows)
    r = np.arange(rows)
    twist = (2 * ids[:, None] + 1) * r[None, :] * (np.pi / (2 * blocks * rows))
    inner = r[:, None] * r[None, :] % rows * (2 * np.pi / rows)
    c, s = np.cos(inner), np.sin(inner)
    full = np.concatenate(
        [np.concatenate([c, -s], axis=1), np.concatenate([s, c], axis=1)], axis=0
    )
    return (
        np.stack(split_table(outer)),
        np.stack(split_table(full)),
        np.stack(split_table(final)),
        np.stack([np.cos(twist), np.sin(twist)]).astype(np.float32),
    )


def mm(left, right):
    return jnp.dot(left, right, preferred_element_type=F32)


def halves(x):
    high = x.astype(BF16)
    return high, (x - high.astype(F32)).astype(BF16)


def mm3(left, right_ref):
    high, low = halves(left)
    return mm(high, right_ref[0]) + mm(low, right_ref[0]) + mm(high, right_ref[1])


def kernel(
    blocks, lanes,
    values_hbm, gates_hbm, taps_hbm, skip_hbm, weight_hbm,
    outer_hbm, full_hbm, final_hbm, twist_hbm,
    out_hbm,
    values_ref, gates_ref, taps_ref, skip_ref, weight_ref,
    outer_ref, full_ref, final_ref, twist_ref,
    sbuf, rbuf, xf, yf, obuf, cbuf, gt, wt, pbuf, qbuf, fin,
    load_sem, send1, recv1, send2, recv2, send3, recv3, own_sem,
):
    me = lax.axis_index("seq")
    mine = lax.axis_index("chan")
    rows, width = values_ref.shape
    narrow = width // blocks

    loads = []
    for index, (source, target) in enumerate(
        (
            (values_hbm, values_ref),
            (taps_hbm, taps_ref),
            (gates_hbm, gates_ref),
            (skip_hbm, skip_ref),
            (weight_hbm, weight_ref),
            (outer_hbm, outer_ref),
            (full_hbm, full_ref),
            (final_hbm, final_ref),
            (twist_hbm, twist_ref),
        )
    ):
        copy = pltpu.make_async_copy(source, target, load_sem.at[index])
        copy.start()
        loads.append(copy)

    barrier = pltpu.get_barrier_semaphore()

    def greet_seq(step, carry):
        pl.semaphore_signal(
            barrier, inc=1, device_id=(lax.rem(me + step, blocks), mine), device_id_type=MESH
        )
        return carry

    def greet_chan(step, carry):
        pl.semaphore_signal(
            barrier, inc=1, device_id=(me, lax.rem(mine + step, lanes)), device_id_type=MESH
        )
        return carry

    lax.fori_loop(1, blocks, greet_seq, 0)
    lax.fori_loop(1, lanes, greet_chan, 0)

    part = 256
    row_ids = lax.broadcasted_iota(jnp.int32, (part, part), 0)
    col_ids = lax.broadcasted_iota(jnp.int32, (part, part), 1)
    eye = jnp.where(row_ids == col_ids, 1.0, 0.0).astype(BF16)

    def turned(block):
        return lax.dot_general(eye, block, (((1,), (1,)), ((), ())), preferred_element_type=F32)

    loads[0].wait()
    loads[1].wait()
    per = part // narrow
    for b in range(width // part):
        columns = slice(b * part, (b + 1) * part)
        v = turned(values_ref[:, columns])
        h = turned(taps_ref[:, columns])
        both = jnp.concatenate(
            [v.reshape(per, narrow, rows), h.reshape(per, narrow, rows)], axis=1
        )
        sbuf[b * per : (b + 1) * per] = both.astype(BF16)

    pl.semaphore_wait(barrier, blocks + lanes - 2)

    def send_first(step, carry):
        peer = lax.rem(me + step, blocks)
        pltpu.make_async_remote_copy(
            src_ref=sbuf.at[peer], dst_ref=rbuf.at[me], send_sem=send1, recv_sem=recv1,
            device_id=(peer, mine), device_id_type=MESH,
        ).start()
        return carry

    lax.fori_loop(1, blocks, send_first, 0)
    own = pltpu.make_async_copy(sbuf.at[me], rbuf.at[me], own_sem.at[0])
    own.start()

    loads[2].wait()
    for b in range(width // part):
        columns = slice(b * part, (b + 1) * part)
        gt[columns, :] = turned(gates_ref[:, columns])
    loads[4].wait()
    for j in range(lanes):
        wt[j] = turned(weight_ref[:, j * part : (j + 1) * part]).astype(BF16)
    for index in (3, 5, 6, 7, 8):
        loads[index].wait()

    own.wait()
    rest = pl.ds(0, blocks - 1)
    pltpu.make_async_copy(rbuf.at[rest], rbuf.at[rest], recv1).wait()

    arrived = rbuf[...].astype(F32).reshape(blocks * 2 * narrow, rows)
    lane = rows // 2
    xf[0] = arrived[:, :lane]
    xf[1] = arrived[:, lane:]
    cos_t, sin_t = twist_ref[0], twist_ref[1]
    cos_2 = jnp.concatenate([cos_t, cos_t], axis=1)
    sin_2 = jnp.concatenate([sin_t, sin_t], axis=1)
    group = narrow // 2
    lines = group * blocks

    def half(g, carry):
        streams = ([], [])
        for c in range(group):
            channel = g * group + c
            x = jnp.concatenate(
                [
                    xf[side, pl.ds(start + channel, blocks, stride=2 * narrow), :]
                    for start in (0, narrow)
                    for side in range(2)
                ],
                axis=1,
            ).astype(BF16)
            y = mm(outer_ref[0], x) + mm(outer_ref[1], x)
            re, im = y[:blocks], y[blocks:]
            real = re * cos_2 + im * sin_2
            imag = im * cos_2 - re * sin_2
            for stream in range(2):
                cut = slice(stream * rows, (stream + 1) * rows)
                streams[stream].append(jnp.concatenate([real[:, cut], imag[:, cut]], axis=1))
        spectra = mm3(jnp.concatenate(streams[0] + streams[1], axis=0), full_ref)
        vre, vim = spectra[:lines, :rows], spectra[:lines, rows:]
        direct = [
            jnp.broadcast_to(skip_ref[pl.ds(me * narrow + g * group + c, 1), :], (blocks, rows))
            for c in range(group)
        ]
        hre = spectra[lines:, :rows] + jnp.concatenate(direct, axis=0)
        him = spectra[lines:, rows:]
        product = jnp.concatenate([vre * hre - vim * him, -(vre * him + vim * hre)], axis=1)
        back = mm3(product, full_ref)
        wide = []
        for c in range(group):
            cut = slice(c * blocks, (c + 1) * blocks)
            re, im = back[cut, :rows], -back[cut, rows:]
            wide.append(
                jnp.concatenate([re * cos_t - im * sin_t, im * cos_t + re * sin_t], axis=0)
            )
        high, low = halves(jnp.concatenate(wide, axis=1))
        signal = mm(final_ref[0], high) + mm(final_ref[0], low) + mm(final_ref[1], high)
        for c in range(group):
            for side in range(2):
                start = c * rows + side * lane
                yf[side, pl.ds(g * group + c, blocks, stride=narrow), :] = signal[
                    :, start : start + lane
                ]
        return carry

    lax.fori_loop(0, 2, half, 0)
    result = jnp.concatenate([yf[0], yf[1]], axis=1)
    obuf[...] = result.reshape(blocks, narrow, rows).astype(BF16)

    def send_second(step, carry):
        peer = lax.rem(me + step, blocks)
        pltpu.make_async_remote_copy(
            src_ref=obuf.at[peer], dst_ref=cbuf.at[me], send_sem=send2, recv_sem=recv2,
            device_id=(peer, mine), device_id_type=MESH,
        ).start()
        return carry

    lax.fori_loop(1, blocks, send_second, 0)
    own = pltpu.make_async_copy(obuf.at[me], cbuf.at[me], own_sem.at[1])
    own.start()
    own.wait()
    pltpu.make_async_copy(cbuf.at[rest], cbuf.at[rest], recv2).wait()

    conv = cbuf[...].astype(F32).reshape(width, rows)
    gated = (gt[...] * conv).astype(BF16)

    def send_third(step, carry):
        peer = lax.rem(mine + step, lanes)
        pbuf[peer] = mm(wt[peer], gated).astype(BF16)
        pltpu.make_async_remote_copy(
            src_ref=pbuf.at[peer], dst_ref=qbuf.at[mine], send_sem=send3, recv_sem=recv3,
            device_id=(me, peer), device_id_type=MESH,
        ).start()
        return carry

    lax.fori_loop(1, lanes, send_third, 0)
    total = mm(wt[mine], gated)
    others = pl.ds(0, lanes - 1)
    pltpu.make_async_copy(qbuf.at[others], qbuf.at[others], recv3).wait()

    def add(step, running):
        return running + qbuf[lax.rem(mine + step, lanes)].astype(F32)

    for step in range(1, lanes):
        total = add(step, total)
    fin[...] = total.astype(BF16)
    done = pltpu.make_async_copy(fin, out_hbm, own_sem.at[2])
    done.start()
    pltpu.make_async_copy(sbuf.at[rest], sbuf.at[rest], send1).wait()
    pltpu.make_async_copy(obuf.at[rest], obuf.at[rest], send2).wait()
    pltpu.make_async_copy(pbuf.at[others], pbuf.at[others], send3).wait()
    done.wait()


def local(blocks, lanes, values, gates, taps, skip, weight):
    rows, width = values.shape
    depth, features = weight.shape
    narrow = width // blocks
    outer, full, final, twist = tables(blocks, rows)
    anywhere = pl.BlockSpec(memory_space=pl.ANY)
    vmem = pltpu.VMEM
    dma = pltpu.SemaphoreType.DMA
    operands = (values, gates, taps, skip[:, None], weight, outer, full, final, twist)
    return pl.pallas_call(
        functools.partial(kernel, blocks, lanes),
        out_shape=jax.ShapeDtypeStruct((features // lanes, rows), BF16),
        in_specs=[anywhere] * len(operands),
        out_specs=anywhere,
        scratch_shapes=[
            vmem(values.shape, BF16),
            vmem(gates.shape, BF16),
            vmem(taps.shape, BF16),
            vmem((width, 1), F32),
            vmem(weight.shape, BF16),
            vmem(outer.shape, BF16),
            vmem(full.shape, BF16),
            vmem(final.shape, BF16),
            vmem(twist.shape, F32),
            vmem((blocks, 2 * narrow, rows), BF16),
            vmem((blocks, 2 * narrow, rows), BF16),
            vmem((2, blocks * 2 * narrow, rows // 2), F32),
            vmem((2, blocks * narrow, rows // 2), F32),
            vmem((blocks, narrow, rows), BF16),
            vmem((blocks, narrow, rows), BF16),
            vmem((width, rows), F32),
            vmem((lanes, features // lanes, depth), BF16),
            vmem((lanes, features // lanes, rows), BF16),
            vmem((lanes, features // lanes, rows), BF16),
            vmem((features // lanes, rows), BF16),
            dma((9,)), dma, dma, dma, dma, dma, dma, dma((3,)),
        ],
        compiler_params=pltpu.CompilerParams(
            collective_id=0, has_side_effects=True, vmem_limit_bytes=56 * 2**20
        ),
        name="hyena",
    )(*operands)


def solution(mesh):
    placed = (P("seq", "chan"), P("seq", "chan"), P("seq", "chan"), P("chan"), P("chan", None))
    body = functools.partial(local, mesh.shape["seq"], mesh.shape["chan"])
    return jax.shard_map(
        body, mesh=mesh, in_specs=placed, out_specs=P("chan", "seq"), check_vma=False
    )
```

```python
import functools

import jax
import jax.numpy as jnp
import numpy as np
from jax import lax
from jax.experimental import pallas as pl
from jax.experimental.pallas import tpu as pltpu
from jax.sharding import PartitionSpec as P

MESH = pl.DeviceIdType.MESH
F32 = jnp.float32
BF16 = jnp.bfloat16


def split_table(table):
    high = table.astype(np.float32).astype(BF16)
    low = (table - high.astype(np.float64)).astype(np.float32).astype(BF16)
    return high, low


def tables(blocks, rows):
    ids = np.arange(blocks)
    turn = ids[:, None] * (2 * ids[None, :] + 1) % (4 * blocks) * (2 * np.pi / (4 * blocks))
    outer = np.concatenate([np.cos(turn).T, -np.sin(turn).T], axis=0)
    final = np.concatenate([np.cos(turn), -np.sin(turn)], axis=1) / (blocks * rows)
    r = np.arange(rows)
    twist = (2 * ids[:, None] + 1) * r[None, :] * (np.pi / (2 * blocks * rows))
    inner = r[:, None] * r[None, :] % rows * (2 * np.pi / rows)
    c, s = np.cos(inner), np.sin(inner)
    full = np.concatenate(
        [np.concatenate([c, -s], axis=1), np.concatenate([s, c], axis=1)], axis=0
    )
    return (
        np.stack(split_table(outer)),
        np.stack(split_table(full)),
        np.stack(split_table(final)),
        np.stack([np.cos(twist), np.sin(twist)]).astype(np.float32),
    )


def mm(left, right):
    return jnp.dot(left, right, preferred_element_type=F32)


def halves(x):
    high = x.astype(BF16)
    return high, (x - high.astype(F32)).astype(BF16)


def mm3(left, right_ref):
    high, low = halves(left)
    return mm(high, right_ref[0]) + mm(low, right_ref[0]) + mm(high, right_ref[1])


def kernel(
    blocks, lanes,
    values_hbm, gates_hbm, taps_hbm, skip_ref, weight_hbm,
    outer_hbm, full_hbm, final_hbm, twist_hbm,
    out_hbm,
    values_ref, gates_ref, taps_ref, weight_ref,
    outer_ref, full_ref, final_ref, twist_ref,
    sbuf, rbuf, xf, yf, obuf, cbuf, gt, wt, pbuf, qbuf, fin,
    load_sem, send1, recv1, send2, recv2, send3, recv3, own_sem,
):
    me = lax.axis_index("seq")
    mine = lax.axis_index("chan")
    rows, width = values_ref.shape
    narrow = width // blocks

    loads = []
    for index, (source, target) in enumerate(
        (
            (values_hbm, values_ref),
            (taps_hbm, taps_ref),
            (gates_hbm, gates_ref),
            (weight_hbm, weight_ref),
            (outer_hbm, outer_ref),
            (full_hbm, full_ref),
            (final_hbm, final_ref),
            (twist_hbm, twist_ref),
        )
    ):
        copy = pltpu.make_async_copy(source, target, load_sem.at[index])
        copy.start()
        loads.append(copy)

    barrier = pltpu.get_barrier_semaphore()

    def greet_seq(step, carry):
        pl.semaphore_signal(
            barrier, inc=1, device_id=(lax.rem(me + step, blocks), mine), device_id_type=MESH
        )
        return carry

    def greet_chan(step, carry):
        pl.semaphore_signal(
            barrier, inc=1, device_id=(me, lax.rem(mine + step, lanes)), device_id_type=MESH
        )
        return carry

    lax.fori_loop(1, blocks, greet_seq, 0)
    lax.fori_loop(1, lanes, greet_chan, 0)

    part = 256
    row_ids = lax.broadcasted_iota(jnp.int32, (part, part), 0)
    col_ids = lax.broadcasted_iota(jnp.int32, (part, part), 1)
    eye = jnp.where(row_ids == col_ids, 1.0, 0.0).astype(BF16)

    def turned(block):
        return lax.dot_general(eye, block, (((1,), (1,)), ((), ())), preferred_element_type=F32)

    loads[0].wait()
    loads[1].wait()
    per = part // narrow
    group = narrow // 2
    row_of = lax.broadcasted_iota(jnp.int32, (per, narrow, rows), 1)

    def paired(first, second):
        low = row_of[: first.shape[0], :, : first.shape[2]] < group
        return (
            jnp.where(low, first, pltpu.roll(second, group, 1)),
            jnp.where(low, pltpu.roll(first, group, 1), second),
        )

    for b in range(width // part):
        columns = slice(b * part, (b + 1) * part)
        v = turned(values_ref[:, columns])
        h = turned(taps_ref[:, columns])
        both = paired(v.reshape(per, narrow, rows), h.reshape(per, narrow, rows))
        for g in range(2):
            sbuf[g, b * per : (b + 1) * per] = both[g].astype(BF16)

    pl.semaphore_wait(barrier, blocks + lanes - 2)

    def exchange(source, target, g, send_sem, recv_sem):
        def send(number, carry):
            step = blocks - number
            hop = lax.rem(step, 2) * ((step + 1) // 2) + (1 - lax.rem(step, 2)) * (
                blocks - step // 2
            )
            peer = lax.rem(me + hop, blocks)
            pltpu.make_async_remote_copy(
                src_ref=source.at[g, peer], dst_ref=target.at[g, me],
                send_sem=send_sem.at[g], recv_sem=recv_sem.at[g],
                device_id=(peer, mine), device_id_type=MESH,
            ).start()
            return carry

        lax.fori_loop(1, blocks, send, 0)

    def all_of(ref, g, sem):
        return pltpu.make_async_copy(ref.at[g, rest], ref.at[g, rest], sem.at[g])

    rest = pl.ds(0, blocks - 1)
    for g in range(2):
        exchange(sbuf, rbuf, g, send1, recv1)
    owns = [
        pltpu.make_async_copy(sbuf.at[g, me], rbuf.at[g, me], own_sem.at[g]) for g in range(2)
    ]
    for own in owns:
        own.start()

    loads[2].wait()
    for b in range(width // part):
        columns = slice(b * part, (b + 1) * part)
        gt[columns, :] = turned(gates_ref[:, columns])
    loads[3].wait()
    for j in range(lanes):
        wt[j] = turned(weight_ref[:, j * part : (j + 1) * part]).astype(BF16)
    for index in (4, 5, 6, 7):
        loads[index].wait()

    for own in owns:
        own.wait()
    lane = rows // 2
    cos_t, sin_t = twist_ref[0], twist_ref[1]
    cos_2 = jnp.concatenate([cos_t, cos_t], axis=1)
    sin_2 = jnp.concatenate([sin_t, sin_t], axis=1)
    lines = group * blocks

    def half(g, carry):
        all_of(rbuf, g, recv1).wait()
        arrived = rbuf[g].astype(F32).reshape(blocks * narrow, rows)
        xf[0] = arrived[:, :lane]
        xf[1] = arrived[:, lane:]
        streams = ([], [])
        for c in range(group):
            x = jnp.concatenate(
                [
                    xf[side, pl.ds(start + c, blocks, stride=narrow), :]
                    for start in (0, group)
                    for side in range(2)
                ],
                axis=1,
            ).astype(BF16)
            y = mm(outer_ref[0], x) + mm(outer_ref[1], x)
            re, im = y[:blocks], y[blocks:]
            real = re * cos_2 + im * sin_2
            imag = im * cos_2 - re * sin_2
            for stream in range(2):
                cut = slice(stream * rows, (stream + 1) * rows)
                streams[stream].append(jnp.concatenate([real[:, cut], imag[:, cut]], axis=1))
        spectra = mm3(jnp.concatenate(streams[0] + streams[1], axis=0), full_ref)
        vre, vim = spectra[:lines, :rows], spectra[:lines, rows:]
        direct = [
            jnp.full((blocks, rows), skip_ref[me * narrow + g * group + c], F32)
            for c in range(group)
        ]
        hre = spectra[lines:, :rows] + jnp.concatenate(direct, axis=0)
        him = spectra[lines:, rows:]
        product = jnp.concatenate([vre * hre - vim * him, -(vre * him + vim * hre)], axis=1)
        back = mm3(product, full_ref)
        wide = []
        for c in range(group):
            cut = slice(c * blocks, (c + 1) * blocks)
            re, im = back[cut, :rows], -back[cut, rows:]
            wide.append(
                jnp.concatenate([re * cos_t - im * sin_t, im * cos_t + re * sin_t], axis=0)
            )
        high, low = halves(jnp.concatenate(wide, axis=1))
        signal = mm(final_ref[0], high) + mm(final_ref[0], low) + mm(final_ref[1], high)
        for c in range(group):
            for side in range(2):
                start = c * rows + side * lane
                yf[pl.ds(side * group + c, blocks, stride=narrow), :] = signal[
                    :, start : start + lane
                ]
        obuf[g] = yf[...].reshape(blocks, narrow, lane).astype(BF16)
        exchange(obuf, cbuf, g, send2, recv2)
        return carry

    lax.fori_loop(0, 2, half, 0)
    owns = [
        pltpu.make_async_copy(obuf.at[g, me], cbuf.at[g, me], own_sem.at[2 + g]) for g in range(2)
    ]
    for own in owns:
        own.start()
    for own in owns:
        own.wait()
    for g in range(2):
        all_of(cbuf, g, recv2).wait()

    row_of = lax.broadcasted_iota(jnp.int32, (blocks, narrow, lane), 1)
    conv = jnp.concatenate(
        [
            piece.reshape(width, lane)
            for piece in paired(cbuf[0].astype(F32), cbuf[1].astype(F32))
        ],
        axis=1,
    )
    gated = (gt[...] * conv).astype(BF16)

    def send_third(step, carry):
        peer = lax.rem(mine + step, lanes)
        pbuf[peer] = mm(wt[peer], gated).astype(BF16)
        pltpu.make_async_remote_copy(
            src_ref=pbuf.at[peer], dst_ref=qbuf.at[mine], send_sem=send3, recv_sem=recv3,
            device_id=(me, peer), device_id_type=MESH,
        ).start()
        return carry

    lax.fori_loop(1, lanes, send_third, 0)
    total = mm(wt[mine], gated)
    others = pl.ds(0, lanes - 1)
    pltpu.make_async_copy(qbuf.at[others], qbuf.at[others], recv3).wait()

    def add(step, running):
        return running + qbuf[lax.rem(mine + step, lanes)].astype(F32)

    for step in range(1, lanes):
        total = add(step, total)
    fin[...] = total.astype(BF16)
    done = pltpu.make_async_copy(fin, out_hbm, own_sem.at[4])
    done.start()
    for g in range(2):
        all_of(sbuf, g, send1).wait()
        all_of(obuf, g, send2).wait()
    pltpu.make_async_copy(pbuf.at[others], pbuf.at[others], send3).wait()
    done.wait()


def local(blocks, lanes, values, gates, taps, skip, weight):
    rows, width = values.shape
    depth, features = weight.shape
    narrow = width // blocks
    outer, full, final, twist = tables(blocks, rows)
    anywhere = pl.BlockSpec(memory_space=pl.ANY)
    vmem = pltpu.VMEM
    dma = pltpu.SemaphoreType.DMA
    operands = (values, gates, taps, skip, weight, outer, full, final, twist)
    return pl.pallas_call(
        functools.partial(kernel, blocks, lanes),
        out_shape=jax.ShapeDtypeStruct((features // lanes, rows), BF16),
        in_specs=[anywhere] * 3 + [pl.BlockSpec(memory_space=pltpu.SMEM)] + [anywhere] * 5,
        out_specs=anywhere,
        scratch_shapes=[
            vmem(values.shape, BF16),
            vmem(gates.shape, BF16),
            vmem(taps.shape, BF16),
            vmem(weight.shape, BF16),
            vmem(outer.shape, BF16),
            vmem(full.shape, BF16),
            vmem(final.shape, BF16),
            vmem(twist.shape, F32),
            vmem((2, blocks, narrow, rows), BF16),
            vmem((2, blocks, narrow, rows), BF16),
            vmem((2, blocks * narrow, rows // 2), F32),
            vmem((blocks * narrow, rows // 2), F32),
            vmem((2, blocks, narrow, rows // 2), BF16),
            vmem((2, blocks, narrow, rows // 2), BF16),
            vmem((width, rows), F32),
            vmem((lanes, features // lanes, depth), BF16),
            vmem((lanes, features // lanes, rows), BF16),
            vmem((lanes, features // lanes, rows), BF16),
            vmem((features // lanes, rows), BF16),
            dma((8,)), dma((2,)), dma((2,)), dma((2,)), dma((2,)), dma, dma, dma((5,)),
        ],
        compiler_params=pltpu.CompilerParams(
            collective_id=0, has_side_effects=True, vmem_limit_bytes=56 * 2**20
        ),
        name="hyena",
    )(*operands)


def solution(mesh):
    placed = (P("seq", "chan"), P("seq", "chan"), P("seq", "chan"), P("chan"), P("chan", None))
    body = functools.partial(local, mesh.shape["seq"], mesh.shape["chan"])
    return jax.shard_map(
        body, mesh=mesh, in_specs=placed, out_specs=P("chan", "seq"), check_vma=False
    )
```

```python
import functools

import jax
import jax.numpy as jnp
import numpy as np
from jax import lax
from jax.experimental import pallas as pl
from jax.experimental.pallas import tpu as pltpu
from jax.sharding import PartitionSpec as P

MESH = pl.DeviceIdType.MESH
F32 = jnp.float32
BF16 = jnp.bfloat16


def split_table(table):
    high = table.astype(np.float32).astype(BF16)
    low = (table - high.astype(np.float64)).astype(np.float32).astype(BF16)
    return high, low


def tables(blocks, rows):
    ids = np.arange(blocks)
    turn = ids[:, None] * (2 * ids[None, :] + 1) % (4 * blocks) * (2 * np.pi / (4 * blocks))
    outer = np.concatenate([np.cos(turn).T, -np.sin(turn).T], axis=0)
    final = np.concatenate([np.cos(turn), -np.sin(turn)], axis=1) / (blocks * rows)
    r = np.arange(rows)
    twist = (2 * ids[:, None] + 1) * r[None, :] * (np.pi / (2 * blocks * rows))
    inner = r[:, None] * r[None, :] % rows * (2 * np.pi / rows)
    c, s = np.cos(inner), np.sin(inner)
    full = np.concatenate(
        [np.concatenate([c, -s], axis=1), np.concatenate([s, c], axis=1)], axis=0
    )
    return (
        np.stack(split_table(outer)),
        np.stack(split_table(full)),
        np.stack(split_table(final)),
        np.stack([np.cos(twist), np.sin(twist)]).astype(np.float32),
    )


def mm(left, right):
    return jnp.dot(left, right, preferred_element_type=F32)


def halves(x):
    high = x.astype(BF16)
    return high, (x - high.astype(F32)).astype(BF16)


def mm3(left, right_ref):
    high, low = halves(left)
    return mm(high, right_ref[0]) + mm(low, right_ref[0]) + mm(high, right_ref[1])


def kernel(
    blocks, lanes,
    values_hbm, gates_hbm, taps_hbm, skip_ref, weight_hbm,
    outer_hbm, full_hbm, final_hbm, twist_hbm,
    out_ref,
    values_ref, gates_ref, taps_ref, weight_ref,
    outer_ref, full_ref, final_ref, twist_ref,
    sbuf, rbuf, xf, yf, obuf, cbuf, gt, wall, wsib, gated, gsib, acc, ubuf, tbuf,
    load_sem, send1, recv1, send2, recv2, pair_send, pair_recv, send4, recv4, own_sem,
):
    me = lax.axis_index("seq")
    mine = lax.axis_index("chan")
    rows, width = values_ref.shape
    rows_out = out_ref.shape[0]
    narrow = width // blocks

    loads = []
    for index, (source, target) in enumerate(
        (
            (values_hbm, values_ref),
            (taps_hbm, taps_ref),
            (gates_hbm, gates_ref),
            (weight_hbm, weight_ref),
            (outer_hbm, outer_ref),
            (full_hbm, full_ref),
            (final_hbm, final_ref),
            (twist_hbm, twist_ref),
        )
    ):
        copy = pltpu.make_async_copy(source, target, load_sem.at[index])
        copy.start()
        loads.append(copy)

    barrier = pltpu.get_barrier_semaphore()

    def greet_seq(step, carry):
        pl.semaphore_signal(
            barrier, inc=1, device_id=(lax.rem(me + step, blocks), mine), device_id_type=MESH
        )
        return carry

    def greet_chan(step, carry):
        pl.semaphore_signal(
            barrier, inc=1, device_id=(me, lax.rem(mine + step, lanes)), device_id_type=MESH
        )
        return carry

    lax.fori_loop(1, blocks, greet_seq, 0)
    lax.fori_loop(1, lanes, greet_chan, 0)

    part = 256
    row_ids = lax.broadcasted_iota(jnp.int32, (part, part), 0)
    col_ids = lax.broadcasted_iota(jnp.int32, (part, part), 1)
    eye = jnp.where(row_ids == col_ids, 1.0, 0.0).astype(BF16)

    def turned(block):
        return lax.dot_general(eye, block, (((1,), (1,)), ((), ())), preferred_element_type=F32)

    loads[0].wait()
    loads[1].wait()
    per = part // narrow
    group = narrow // 2
    row_of = lax.broadcasted_iota(jnp.int32, (per, narrow, rows), 1)

    def paired(first, second):
        low = row_of[: first.shape[0], :, : first.shape[2]] < group
        return (
            jnp.where(low, first, pltpu.roll(second, group, 1)),
            jnp.where(low, pltpu.roll(first, group, 1), second),
        )

    for g in range(2):
        columns = slice(g * part, (g + 1) * part)
        v = turned(values_ref[:, columns]).reshape(per, narrow, rows)
        h = turned(taps_ref[:, columns]).reshape(per, narrow, rows)
        both = jnp.stack(paired(v, h), axis=1).reshape(blocks, narrow, rows)
        sbuf[g] = both.astype(BF16)

    pl.semaphore_wait(barrier, blocks + lanes - 2)

    def exchange(source, target, send_sem, recv_sem):
        def send(hop):
            peer = me + hop
            peer = jnp.where(peer >= blocks, peer - blocks, peer)
            pltpu.make_async_remote_copy(
                src_ref=source.at[peer], dst_ref=target.at[me],
                send_sem=send_sem, recv_sem=recv_sem,
                device_id=(peer, mine), device_id_type=MESH,
            ).start()

        def pair(step, carry):
            send(blocks // 2 - step)
            send(blocks // 2 + step)
            return carry

        send(blocks // 2)
        lax.fori_loop(1, blocks // 2, pair, 0)

    def all_of(ref, sem):
        return pltpu.make_async_copy(ref.at[rest], ref.at[rest], sem)

    rest = pl.ds(0, blocks - 1)
    for g in range(2):
        exchange(sbuf.at[g], rbuf.at[g], send1.at[g], recv1.at[g])
    owns = [
        pltpu.make_async_copy(sbuf.at[g, me], rbuf.at[g, me], own_sem.at[g]) for g in range(2)
    ]
    for own in owns:
        own.start()

    chips = lanes // 2
    chip = mine // 2
    core = lax.rem(mine, 2)
    sibling = (me, 2 * chip + 1 - core)

    loads[2].wait()
    for g in range(2):
        columns = slice(g * part, (g + 1) * part)
        gt[g] = turned(gates_ref[:, columns])
    loads[3].wait()
    for j in range(lanes):
        wall[j % 2, j // 2] = turned(weight_ref[:, j * part : (j + 1) * part]).astype(BF16)
    pltpu.make_async_remote_copy(
        src_ref=wall.at[1 - core], dst_ref=wsib, send_sem=pair_send.at[2],
        recv_sem=pair_recv.at[2], device_id=sibling, device_id_type=MESH,
    ).start()
    for index in (4, 5, 6, 7):
        loads[index].wait()

    for own in owns:
        own.wait()
    lane = rows // 2
    cos_t, sin_t = twist_ref[0], twist_ref[1]
    cos_2 = jnp.concatenate([cos_t, cos_t], axis=1)
    sin_2 = jnp.concatenate([sin_t, sin_t], axis=1)
    lines = group * blocks

    def half(g, carry):
        all_of(rbuf.at[g], recv1.at[g]).wait()
        arrived = rbuf[g].astype(F32).reshape(blocks * narrow, rows)
        xf[0] = arrived[:, :lane]
        xf[1] = arrived[:, lane:]
        streams = ([], [])
        for c in range(group):
            x = jnp.concatenate(
                [
                    xf[side, pl.ds(start + c, blocks, stride=narrow), :]
                    for start in (0, group)
                    for side in range(2)
                ],
                axis=1,
            ).astype(BF16)
            y = mm(outer_ref[0], x) + mm(outer_ref[1], x)
            re, im = y[:blocks], y[blocks:]
            real = re * cos_2 + im * sin_2
            imag = im * cos_2 - re * sin_2
            for stream in range(2):
                cut = slice(stream * rows, (stream + 1) * rows)
                streams[stream].append(jnp.concatenate([real[:, cut], imag[:, cut]], axis=1))
        spectra = mm3(jnp.concatenate(streams[0] + streams[1], axis=0), full_ref)
        vre, vim = spectra[:lines, :rows], spectra[:lines, rows:]
        direct = [
            jnp.full((blocks, rows), skip_ref[g * part + me * group + c], F32)
            for c in range(group)
        ]
        hre = spectra[lines:, :rows] + jnp.concatenate(direct, axis=0)
        him = spectra[lines:, rows:]
        product = jnp.concatenate([vre * hre - vim * him, -(vre * him + vim * hre)], axis=1)
        back = mm3(product, full_ref)
        wide = []
        for c in range(group):
            cut = slice(c * blocks, (c + 1) * blocks)
            re, im = back[cut, :rows], -back[cut, rows:]
            wide.append(
                jnp.concatenate([re * cos_t - im * sin_t, im * cos_t + re * sin_t], axis=0)
            )
        high, low = halves(jnp.concatenate(wide, axis=1))
        signal = mm(final_ref[0], high) + mm(final_ref[0], low) + mm(final_ref[1], high)
        for c in range(group):
            for side in range(2):
                start = c * rows + side * lane
                yf[pl.ds(side * group + c, blocks, stride=narrow), :] = signal[
                    :, start : start + lane
                ]
        obuf[g] = yf[...].reshape(blocks, narrow, lane).astype(BF16)
        exchange(obuf.at[g], cbuf.at[g], send2.at[g], recv2.at[g])
        return carry

    lax.fori_loop(0, 2, half, 0)
    owns = [
        pltpu.make_async_copy(obuf.at[g, me], cbuf.at[g, me], own_sem.at[2 + g]) for g in range(2)
    ]
    for own in owns:
        own.start()
    for own in owns:
        own.wait()

    pair_copies = []
    order = [2, 1, 3, 0]
    row_of = lax.broadcasted_iota(jnp.int32, (per, narrow, lane), 1)
    for g in range(2):
        all_of(cbuf.at[g], recv2.at[g]).wait()
        back = cbuf[g].astype(F32).reshape(per, 2, narrow, lane)
        pieces = paired(back[:, 0], back[:, 1])
        conv = jnp.concatenate([piece.reshape(part, lane) for piece in pieces], axis=1)
        gated[g] = (gt[g] * conv).astype(BF16)
        copy = pltpu.make_async_remote_copy(
            src_ref=gated.at[g], dst_ref=gsib.at[g], send_sem=pair_send.at[g],
            recv_sem=pair_recv.at[g], device_id=sibling, device_id_type=MESH,
        )
        copy.start()
        pair_copies.append(copy)
        columns = slice(g * part, (g + 1) * part)
        for hop in order:
            there = lax.rem(chip + hop, chips)
            term = mm(wall[core, there, :, columns], gated[g])
            acc[hop] = term if g == 0 else acc[hop] + term
        if g == 0:
            pltpu.make_async_copy(wsib, wsib, pair_recv.at[2]).wait()
            copy.wait_recv()
            for hop in order:
                there = lax.rem(chip + hop, chips)
                acc[hop] = acc[hop] + mm(wsib[there, :, columns], gsib[g])
    columns = slice(part, 2 * part)
    pair_copies[1].wait_recv()
    middle = rows_out // 2
    own_half = [slice(0, middle), slice(middle, rows_out)]

    def pass_on(way, stage, value, target):
        ubuf[way, stage] = value.astype(BF16)
        there = lax.rem(chip + (1, chips - 1)[way], chips)
        pltpu.make_async_remote_copy(
            src_ref=ubuf.at[way, stage], dst_ref=target, send_sem=send4,
            recv_sem=recv4.at[way, stage], device_id=(me, 2 * there + core),
            device_id_type=MESH,
        ).start()

    def came(way, stage, ref):
        pltpu.make_async_copy(ref, ref, recv4.at[way, stage]).wait()

    def finished(hop):
        there = lax.rem(chip + hop, chips)
        return acc[hop] + mm(wsib[there, :, columns], gsib[1])

    far = finished(2)
    for way in range(2):
        pass_on(way, 0, far[own_half[way]], tbuf.at[way, 0])
    near = []
    for way, hop in ((0, 1), (1, 3)):
        near.append(finished(hop))
        pass_on(way, 1, near[way][own_half[1 - way]], tbuf.at[way, 1])
    total = finished(0)
    for way in range(2):
        came(way, 0, tbuf.at[way, 0])
        merged = near[way][own_half[way]] + tbuf[way, 0].astype(F32)
        pass_on(way, 2, merged, tbuf.at[way, 2])
    for way in range(2):
        came(way, 1, tbuf.at[way, 1])
    for way in range(2):
        came(way, 2, tbuf.at[way, 2])
        out_ref[own_half[way], :] = (
            total[own_half[way]] + tbuf[way, 2].astype(F32) + tbuf[1 - way, 1].astype(F32)
        ).astype(out_ref.dtype)
    for g in range(2):
        all_of(sbuf.at[g], send1.at[g]).wait()
        all_of(obuf.at[g], send2.at[g]).wait()
        pair_copies[g].wait_send()
    pltpu.make_async_copy(wsib, wsib, pair_send.at[2]).wait()
    pltpu.make_async_copy(ubuf, ubuf, send4).wait()


def local(blocks, lanes, values, gates, taps, skip, weight):
    rows, width = values.shape
    depth, features = weight.shape
    narrow = width // blocks
    outer, full, final, twist = tables(blocks, rows)
    anywhere = pl.BlockSpec(memory_space=pl.ANY)
    vmem = pltpu.VMEM
    dma = pltpu.SemaphoreType.DMA
    operands = (values, gates, taps, skip, weight, outer, full, final, twist)
    return pl.pallas_call(
        functools.partial(kernel, blocks, lanes),
        out_shape=jax.ShapeDtypeStruct((features // lanes, rows), BF16),
        in_specs=[anywhere] * 3 + [pl.BlockSpec(memory_space=pltpu.SMEM)] + [anywhere] * 5,
        out_specs=pl.BlockSpec(memory_space=pltpu.VMEM),
        scratch_shapes=[
            vmem(values.shape, BF16),
            vmem(gates.shape, BF16),
            vmem(taps.shape, BF16),
            vmem(weight.shape, BF16),
            vmem(outer.shape, BF16),
            vmem(full.shape, BF16),
            vmem(final.shape, BF16),
            vmem(twist.shape, F32),
            vmem((2, blocks, narrow, rows), BF16),
            vmem((2, blocks, narrow, rows), BF16),
            vmem((2, blocks * narrow, rows // 2), F32),
            vmem((blocks * narrow, rows // 2), F32),
            vmem((2, blocks, narrow, rows // 2), BF16),
            vmem((2, blocks, narrow, rows // 2), BF16),
            vmem((2, width // 2, rows), F32),
            vmem((2, lanes // 2, features // lanes, depth), BF16),
            vmem((lanes // 2, features // lanes, depth), BF16),
            vmem((2, width // 2, rows), BF16),
            vmem((2, width // 2, rows), BF16),
            vmem((lanes // 2, features // lanes, rows), F32),
            vmem((2, 3, features // lanes // 2, rows), BF16),
            vmem((2, 3, features // lanes // 2, rows), BF16),
            dma((8,)), dma((2,)), dma((2,)), dma((2,)), dma((2,)),
            dma((3,)), dma((3,)), dma, dma((2, 3)), dma((4,)),
        ],
        compiler_params=pltpu.CompilerParams(
            collective_id=0, has_side_effects=True, vmem_limit_bytes=56 * 2**20
        ),
        name="hyena",
    )(*operands)


def solution(mesh):
    placed = (P("seq", "chan"), P("seq", "chan"), P("seq", "chan"), P("chan"), P("chan", None))
    body = functools.partial(local, mesh.shape["seq"], mesh.shape["chan"])
    return jax.shard_map(
        body, mesh=mesh, in_specs=placed, out_specs=P("chan", "seq"), check_vma=False
    )
```

```python
import functools

import jax
import jax.numpy as jnp
import numpy as np
from jax import lax
from jax.experimental import pallas as pl
from jax.experimental.pallas import tpu as pltpu
from jax.sharding import PartitionSpec as P

MESH = pl.DeviceIdType.MESH
F32 = jnp.float32
BF16 = jnp.bfloat16


def split_table(table):
    high = table.astype(np.float32).astype(BF16)
    low = (table - high.astype(np.float64)).astype(np.float32).astype(BF16)
    return high, low


def tables(blocks, rows):
    ids = np.arange(blocks)
    turn = ids[:, None] * (2 * ids[None, :] + 1) % (4 * blocks) * (2 * np.pi / (4 * blocks))
    outer = np.concatenate([np.cos(turn).T, -np.sin(turn).T], axis=0)
    final = np.concatenate([np.cos(turn), -np.sin(turn)], axis=1) / (blocks * rows)
    r = np.arange(rows)
    twist = (2 * ids[:, None] + 1) * r[None, :] * (np.pi / (2 * blocks * rows))
    inner = r[:, None] * r[None, :] % rows * (2 * np.pi / rows)
    c, s = np.cos(inner), np.sin(inner)
    full = np.concatenate(
        [np.concatenate([c, -s], axis=1), np.concatenate([s, c], axis=1)], axis=0
    )
    return (
        np.stack(split_table(outer)),
        np.stack(split_table(full)),
        np.stack(split_table(final)),
        np.stack([np.cos(twist), np.sin(twist)]).astype(np.float32),
    )


def mm(left, right):
    return jnp.dot(left, right, preferred_element_type=F32)


def halves(x):
    high = x.astype(BF16)
    return high, (x - high.astype(F32)).astype(BF16)


def mm3(left, right_ref):
    high, low = halves(left)
    return mm(high, right_ref[0]) + mm(low, right_ref[0]) + mm(high, right_ref[1])


def kernel(
    blocks, lanes,
    values_hbm, gates_hbm, taps_hbm, skip_hbm, weight_hbm,
    outer_hbm, full_hbm, final_hbm, twist_hbm,
    out_ref,
    values_ref, gates_ref, taps_ref, skip_ref, weight_ref,
    outer_ref, full_ref, final_ref, twist_ref,
    sbuf, rbuf, xf, yf, obuf, cbuf, gt, wall, wsib, gated, gsib, acc, ubuf, tbuf,
    load_sem, send1, recv1, send2, recv2, pair_send, pair_recv, send4, recv4, own_sem,
):
    me = lax.axis_index("seq")
    mine = lax.axis_index("chan")
    rows, width = values_ref.shape
    rows_out = out_ref.shape[0]
    narrow = width // blocks

    loads = []
    for index, (source, target) in enumerate(
        (
            (values_hbm, values_ref),
            (taps_hbm, taps_ref),
            (gates_hbm, gates_ref),
            (weight_hbm, weight_ref),
            (outer_hbm, outer_ref),
            (full_hbm, full_ref),
            (final_hbm, final_ref),
            (twist_hbm, twist_ref),
            (skip_hbm, skip_ref),
        )
    ):
        copy = pltpu.make_async_copy(source, target, load_sem.at[index])
        copy.start()
        loads.append(copy)

    barrier = pltpu.get_barrier_semaphore()

    def greet(hop):
        peer = me + hop
        peer = jnp.where(peer >= blocks, peer - blocks, peer)
        pl.semaphore_signal(barrier, inc=1, device_id=(peer, mine), device_id_type=MESH)

    def greet_seq(step, carry):
        greet(blocks // 2 - step)
        greet(blocks // 2 + step)
        return carry

    def greet_chan(step, carry):
        pl.semaphore_signal(
            barrier, inc=1, device_id=(me, lax.rem(mine + step, lanes)), device_id_type=MESH
        )
        return carry

    greet(blocks // 2)
    lax.fori_loop(1, blocks // 2, greet_seq, 0)
    lax.fori_loop(1, lanes, greet_chan, 0)

    part = 256
    row_ids = lax.broadcasted_iota(jnp.int32, (part, part), 0)
    col_ids = lax.broadcasted_iota(jnp.int32, (part, part), 1)
    eye = jnp.where(row_ids == col_ids, 1.0, 0.0).astype(BF16)

    def turned(block):
        return lax.dot_general(eye, block, (((1,), (1,)), ((), ())), preferred_element_type=F32)

    loads[0].wait()
    loads[1].wait()
    per = part // narrow
    group = narrow // 2
    row_of = lax.broadcasted_iota(jnp.int32, (per, narrow, rows), 1)

    def paired(first, second):
        low = row_of[: first.shape[0], :, : first.shape[2]] < group
        return (
            jnp.where(low, first, pltpu.roll(second, group, 1)),
            jnp.where(low, pltpu.roll(first, group, 1), second),
        )

    for g in range(2):
        columns = slice(g * part, (g + 1) * part)
        v = turned(values_ref[:, columns]).reshape(per, narrow, rows)
        h = turned(taps_ref[:, columns]).reshape(per, narrow, rows)
        both = jnp.stack(paired(v, h), axis=1).reshape(blocks, narrow, rows)
        sbuf[g] = both.astype(BF16)

    pl.semaphore_wait(barrier, blocks + lanes - 2)

    def exchange(source, target, send_sem, recv_sem):
        def send(hop):
            peer = me + hop
            peer = jnp.where(peer >= blocks, peer - blocks, peer)
            pltpu.make_async_remote_copy(
                src_ref=source.at[peer], dst_ref=target.at[me],
                send_sem=send_sem, recv_sem=recv_sem,
                device_id=(peer, mine), device_id_type=MESH,
            ).start()

        def pair(step, carry):
            send(blocks // 2 - step)
            send(blocks // 2 + step)
            return carry

        send(blocks // 2)
        lax.fori_loop(1, blocks // 2, pair, 0)

    def all_of(ref, sem):
        return pltpu.make_async_copy(ref.at[rest], ref.at[rest], sem)

    rest = pl.ds(0, blocks - 1)
    for g in range(2):
        exchange(sbuf.at[g], rbuf.at[g], send1.at[g], recv1.at[g])
    owns = [
        pltpu.make_async_copy(sbuf.at[g, me], rbuf.at[g, me], own_sem.at[g]) for g in range(2)
    ]
    for own in owns:
        own.start()

    chips = lanes // 2
    chip = mine // 2
    core = lax.rem(mine, 2)
    sibling = (me, 2 * chip + 1 - core)

    loads[2].wait()
    for g in range(2):
        columns = slice(g * part, (g + 1) * part)
        gt[g] = turned(gates_ref[:, columns])
    loads[3].wait()
    for j in range(lanes):
        wall[j % 2, j // 2] = turned(weight_ref[:, j * part : (j + 1) * part]).astype(BF16)
    pltpu.make_async_remote_copy(
        src_ref=wall.at[1 - core], dst_ref=wsib, send_sem=pair_send.at[2],
        recv_sem=pair_recv.at[2], device_id=sibling, device_id_type=MESH,
    ).start()
    for index in (4, 5, 6, 7, 8):
        loads[index].wait()

    for own in owns:
        own.wait()
    lane = rows // 2
    cos_t, sin_t = twist_ref[0], twist_ref[1]
    cos_2 = jnp.concatenate([cos_t, cos_t], axis=1)
    sin_2 = jnp.concatenate([sin_t, sin_t], axis=1)
    lines = group * blocks

    def half(g, carry):
        all_of(rbuf.at[g], recv1.at[g]).wait()
        arrived = rbuf[g].astype(F32).reshape(blocks * narrow, rows)
        xf[0] = arrived[:, :lane]
        xf[1] = arrived[:, lane:]
        streams = ([], [])
        for c in range(group):
            x = jnp.concatenate(
                [
                    xf[side, pl.ds(start + c, blocks, stride=narrow), :]
                    for start in (0, group)
                    for side in range(2)
                ],
                axis=1,
            ).astype(BF16)
            y = mm(outer_ref[0], x) + mm(outer_ref[1], x)
            re, im = y[:blocks], y[blocks:]
            real = re * cos_2 + im * sin_2
            imag = im * cos_2 - re * sin_2
            for stream in range(2):
                cut = slice(stream * rows, (stream + 1) * rows)
                streams[stream].append(jnp.concatenate([real[:, cut], imag[:, cut]], axis=1))
        spectra = mm3(jnp.concatenate(streams[0] + streams[1], axis=0), full_ref)
        vre, vim = spectra[:lines, :rows], spectra[:lines, rows:]
        direct = [
            jnp.full((blocks, rows), skip_ref[g * part + me * group + c], F32)
            for c in range(group)
        ]
        hre = spectra[lines:, :rows] + jnp.concatenate(direct, axis=0)
        him = spectra[lines:, rows:]
        product = jnp.concatenate([vre * hre - vim * him, -(vre * him + vim * hre)], axis=1)
        back = mm3(product, full_ref)
        wide = []
        for c in range(group):
            cut = slice(c * blocks, (c + 1) * blocks)
            re, im = back[cut, :rows], -back[cut, rows:]
            wide.append(
                jnp.concatenate([re * cos_t - im * sin_t, im * cos_t + re * sin_t], axis=0)
            )
        high, low = halves(jnp.concatenate(wide, axis=1))
        signal = mm(final_ref[0], high) + mm(final_ref[0], low) + mm(final_ref[1], high)
        for c in range(group):
            for side in range(2):
                start = c * rows + side * lane
                yf[pl.ds(side * group + c, blocks, stride=narrow), :] = signal[
                    :, start : start + lane
                ]
        obuf[g] = yf[...].reshape(blocks, narrow, lane).astype(BF16)
        exchange(obuf.at[g], cbuf.at[g], send2.at[g], recv2.at[g])
        return carry

    lax.fori_loop(0, 2, half, 0)
    owns = [
        pltpu.make_async_copy(obuf.at[g, me], cbuf.at[g, me], own_sem.at[2 + g]) for g in range(2)
    ]
    for own in owns:
        own.start()
    for own in owns:
        own.wait()

    pair_copies = []
    order = [2, 1, 3, 0]
    row_of = lax.broadcasted_iota(jnp.int32, (per, narrow, lane), 1)
    for g in range(2):
        all_of(cbuf.at[g], recv2.at[g]).wait()
        back = cbuf[g].astype(F32).reshape(per, 2, narrow, lane)
        pieces = paired(back[:, 0], back[:, 1])
        conv = jnp.concatenate([piece.reshape(part, lane) for piece in pieces], axis=1)
        gated[g] = (gt[g] * conv).astype(BF16)
        copy = pltpu.make_async_remote_copy(
            src_ref=gated.at[g], dst_ref=gsib.at[g], send_sem=pair_send.at[g],
            recv_sem=pair_recv.at[g], device_id=sibling, device_id_type=MESH,
        )
        copy.start()
        pair_copies.append(copy)
        columns = slice(g * part, (g + 1) * part)
        for hop in order:
            there = lax.rem(chip + hop, chips)
            term = mm(wall[core, there, :, columns], gated[g])
            acc[hop] = term if g == 0 else acc[hop] + term
        if g == 0:
            pltpu.make_async_copy(wsib, wsib, pair_recv.at[2]).wait()
            copy.wait_recv()
            for hop in order:
                there = lax.rem(chip + hop, chips)
                acc[hop] = acc[hop] + mm(wsib[there, :, columns], gsib[g])
    columns = slice(part, 2 * part)
    pair_copies[1].wait_recv()
    middle = rows_out // 2
    own_half = [slice(0, middle), slice(middle, rows_out)]

    def pass_on(way, stage, value, target):
        ubuf[way, stage] = value.astype(BF16)
        there = lax.rem(chip + (1, chips - 1)[way], chips)
        pltpu.make_async_remote_copy(
            src_ref=ubuf.at[way, stage], dst_ref=target, send_sem=send4,
            recv_sem=recv4.at[way, stage], device_id=(me, 2 * there + core),
            device_id_type=MESH,
        ).start()

    def came(way, stage, ref):
        pltpu.make_async_copy(ref, ref, recv4.at[way, stage]).wait()

    def finished(hop):
        there = lax.rem(chip + hop, chips)
        return acc[hop] + mm(wsib[there, :, columns], gsib[1])

    far = finished(2)
    for way in range(2):
        pass_on(way, 0, far[own_half[way]], tbuf.at[way, 0])
    near = []
    for way, hop in ((0, 1), (1, 3)):
        near.append(finished(hop))
        pass_on(way, 1, near[way][own_half[1 - way]], tbuf.at[way, 1])
    total = finished(0)
    for way in range(2):
        came(way, 0, tbuf.at[way, 0])
        merged = near[way][own_half[way]] + tbuf[way, 0].astype(F32)
        pass_on(way, 2, merged, tbuf.at[way, 2])
    for way in range(2):
        came(way, 1, tbuf.at[way, 1])
    for way in range(2):
        came(way, 2, tbuf.at[way, 2])
        out_ref[own_half[way], :] = (
            total[own_half[way]] + tbuf[way, 2].astype(F32) + tbuf[1 - way, 1].astype(F32)
        ).astype(out_ref.dtype)
    for g in range(2):
        all_of(sbuf.at[g], send1.at[g]).wait()
        all_of(obuf.at[g], send2.at[g]).wait()
        pair_copies[g].wait_send()
    pltpu.make_async_copy(wsib, wsib, pair_send.at[2]).wait()
    pltpu.make_async_copy(ubuf, ubuf, send4).wait()


def local(blocks, lanes, values, gates, taps, skip, weight):
    rows, width = values.shape
    depth, features = weight.shape
    narrow = width // blocks
    outer, full, final, twist = tables(blocks, rows)
    anywhere = pl.BlockSpec(memory_space=pl.ANY)
    vmem = pltpu.VMEM
    dma = pltpu.SemaphoreType.DMA
    operands = (values, gates, taps, skip, weight, outer, full, final, twist)
    return pl.pallas_call(
        functools.partial(kernel, blocks, lanes),
        out_shape=jax.ShapeDtypeStruct((features // lanes, rows), BF16),
        in_specs=[anywhere] * len(operands),
        out_specs=pl.BlockSpec(memory_space=pltpu.VMEM),
        scratch_shapes=[
            vmem(values.shape, BF16),
            vmem(gates.shape, BF16),
            vmem(taps.shape, BF16),
            pltpu.SMEM(skip.shape, F32),
            vmem(weight.shape, BF16),
            vmem(outer.shape, BF16),
            vmem(full.shape, BF16),
            vmem(final.shape, BF16),
            vmem(twist.shape, F32),
            vmem((2, blocks, narrow, rows), BF16),
            vmem((2, blocks, narrow, rows), BF16),
            vmem((2, blocks * narrow, rows // 2), F32),
            vmem((blocks * narrow, rows // 2), F32),
            vmem((2, blocks, narrow, rows // 2), BF16),
            vmem((2, blocks, narrow, rows // 2), BF16),
            vmem((2, width // 2, rows), F32),
            vmem((2, lanes // 2, features // lanes, depth), BF16),
            vmem((lanes // 2, features // lanes, depth), BF16),
            vmem((2, width // 2, rows), BF16),
            vmem((2, width // 2, rows), BF16),
            vmem((lanes // 2, features // lanes, rows), F32),
            vmem((2, 3, features // lanes // 2, rows), BF16),
            vmem((2, 3, features // lanes // 2, rows), BF16),
            dma((9,)), dma((2,)), dma((2,)), dma((2,)), dma((2,)),
            dma((3,)), dma((3,)), dma, dma((2, 3)), dma((4,)),
        ],
        compiler_params=pltpu.CompilerParams(
            collective_id=0, has_side_effects=True, vmem_limit_bytes=56 * 2**20
        ),
        name="hyena",
    )(*operands)


def solution(mesh):
    placed = (P("seq", "chan"), P("seq", "chan"), P("seq", "chan"), P("chan"), P("chan", None))
    body = functools.partial(local, mesh.shape["seq"], mesh.shape["chan"])
    return jax.shard_map(
        body, mesh=mesh, in_specs=placed, out_specs=P("chan", "seq"), check_vma=False
    )
```
